32 devices in a mesh: grp: 1, seq: 32 (over z, y, x, core), head: 1.
Axes of the slice: x: 2, y: 2, z: 4, core: 2. Of those that a mesh axis runs over, the one named last changes fastest.
Arguments:
- queries: bfloat16 [8192, 2048], P(('grp', 'seq'), 'head'), may hold values from -6 to 6
- keys: bfloat16 [8192, 2048], P(('grp', 'seq'), 'head'), may hold values from -6 to 6
- values: bfloat16 [8192, 2048], P(('grp', 'seq'), 'head'), may hold values from -6 to 6
- out_gain: float32 [2048], P('head'), may hold values from 0.4 to 1.6
- hash_ids: int32 [2, 128], replicated, may hold values from 0 to 15
- sign_ids: int32 [2, 128], replicated, may hold values from 0 to 1
Outputs:
- attended: bfloat16 [8192, 2048], P(('grp', 'seq'), 'head')
The draws below stay inside these ranges and needn't reach their ends.
Inputs may be any that keep to these rules, and one draw needn't show every extreme that they name: `hash_ids`: bucket of feature i at each level. `sign_ids`: 1 stands for sign +1, 0 for -1.
All inputs are finite; a program needn't handle non-finite values.
Results may differ from the reference program's by a relative error of at most 0.0056.
Values may be sent and summed in bfloat16 or wider, within the bound.
No kernel may reach another device: no remote copies, remote signals or barrier semaphores. Data moves between devices by JAX's collectives and lax.ppermute only.
A program may use at most 64 MiB of HBM per device.

```python
import jax
import jax.numpy as jnp
from jax import lax

HEADS = 16
HD = 128
BUCKETS = 16
TOK_DEV = 256
TOKENS = 8192


def place_ends(array, rng, low, top_value):
    index_at = [jax.random.randint(jax.random.fold_in(rng, axis), (), 0, length) for axis, length in enumerate(array.shape)]
    widest = array.shape.index(max(array.shape))
    beside = index_at[:widest] + [(index_at[widest] + 1) % array.shape[widest]] + index_at[widest + 1:]
    return array.at[tuple(index_at)].set(low).at[tuple(beside)].set(top_value)


def levels(stream_key, dims, shards, least, largest):
    loudness = 1.0
    for axis_at, parts in shards:
        heights = jax.random.uniform(jax.random.fold_in(jax.random.fold_in(stream_key, 6), axis_at), (parts,), jnp.float32, least / len(shards), largest / len(shards))
        loudness = loudness * jnp.repeat(jnp.exp(heights), dims[axis_at] // parts).reshape((-1,) + (1,) * (len(dims) - 1 - axis_at))
    return loudness


def gaussian(rng, shape, spread, most, cuts=(), held_as=jnp.bfloat16):
    values = jax.random.normal(rng, shape, jnp.float32) * spread
    if len(cuts) > 0:
        values = levels(rng, shape, cuts, -0.22, 0.18) * values
    return jnp.clip(values, min=-most, max=most).astype(held_as)


def setup_inputs(seed: int = 0, part: int = 0) -> dict:
    splits = jax.random.split(jax.random.key(seed), 7)
    own_keys = jax.random.split(jax.random.fold_in(splits[6], part), 7)
    return {
        "queries": gaussian(own_keys[0], (TOKENS, HEADS * HD), 1.0, 6.0, ((0, 32),)),
        "keys": gaussian(own_keys[1], (TOKENS, HEADS * HD), 1.0, 6.0, ((0, 32),)),
        "values": gaussian(own_keys[2], (TOKENS, HEADS * HD), 1.0, 6.0, ((0, 32),)),
        "out_gain": jnp.clip(1.0 + 0.12 * jax.random.normal(splits[3], (HEADS * HD,), jnp.float32), 0.4, 1.6),
        "hash_ids": place_ends(jax.random.randint(splits[4], (2, HD), 0, BUCKETS), jax.random.fold_in(splits[4], 1), 0, BUCKETS - 1).astype(jnp.int32),
        "sign_ids": place_ends(jax.random.randint(splits[5], (2, HD), 0, 2), jax.random.fold_in(splits[5], 1), 0, 1).astype(jnp.int32),
    }


def sketch_matrix(hash_ids, sign_ids):
    buckets = jnp.arange(BUCKETS, dtype=jnp.int32)
    signs = (2 * sign_ids - 1).astype(jnp.float32)
    onehot = (hash_ids[:, :, None] == buckets[None, None, :]).astype(jnp.float32) * signs[:, :, None]
    return jnp.concatenate([onehot[0], onehot[1]], axis=1).astype(jnp.bfloat16)

def features(block, sketch):
    rows = block.reshape(-1, HD)
    factor = 0.75 * (BUCKETS / HD) ** 0.5
    both = jnp.dot(rows, sketch, preferred_element_type=jnp.float32) * factor
    level = both[:, :BUCKETS] * both[:, BUCKETS:]
    outer = level[:, :, None] * level[:, None, :]
    return outer.reshape(block.shape[0], -1, BUCKETS * BUCKETS).astype(jnp.bfloat16)

def near_part(query_blk, key_blk, value_blk, key_prev, value_prev):
    block_rows = query_blk.shape[0]
    heads_here = query_blk.shape[1] // HD
    query_heads = query_blk.reshape(block_rows, heads_here, HD).astype(jnp.float32)
    key_all = jnp.concatenate([key_prev, key_blk], 0).reshape(2 * block_rows, heads_here, HD).astype(jnp.float32)
    value_all = jnp.concatenate([value_prev, value_blk], 0).reshape(2 * block_rows, heads_here, HD).astype(jnp.float32)
    scores = jnp.einsum('qhd,khd->hqk', query_heads, key_all) * float(HD) ** (-0.5)
    rows_index = jnp.arange(block_rows, dtype=jnp.int32)[:, None]
    cols_index = jnp.arange(2 * block_rows, dtype=jnp.int32)[None, :]
    allowed = cols_index <= rows_index + block_rows
    weights = jnp.where(allowed[None], scores ** 4, 0.0).astype(jnp.bfloat16)
    return jnp.einsum('hqk,khd->qhd', weights.astype(jnp.float32), value_all)

def reference(queries, keys, values, out_gain, hash_ids, sign_ids):
    length = queries.shape[0]
    blocks = length // TOK_DEV
    sketch = sketch_matrix(hash_ids, sign_ids)
    query_b = queries.reshape(blocks, TOK_DEV, HEADS * HD)
    key_b = keys.reshape(blocks, TOK_DEV, HEADS * HD)
    value_b = values.reshape(blocks, TOK_DEV, HEADS * HD)
    gain_rows = out_gain.reshape(HEADS, HD)

    def advance(carry, items):
        far_state, prev_total, key_prev, value_prev = carry
        query_blk, key_blk, value_blk = items
        near_sum = near_part(query_blk, key_blk, value_blk, key_prev, value_prev)
        phi_query = features(query_blk, sketch).astype(jnp.float32)
        far_half = far_state.astype(jnp.bfloat16).astype(jnp.float32)
        distant = jnp.einsum('thf,hfd->thd', phi_query, far_half)
        mixed = near_sum + distant
        mean_square = lax.optimization_barrier(jnp.mean(mixed * mixed, axis=-1, keepdims=True))
        normed = mixed * lax.rsqrt(mean_square + 1e-06) * gain_rows[None]
        result = normed.reshape(TOK_DEV, HEADS * HD).astype(jnp.bfloat16)
        phi_key = features(key_blk, sketch).astype(jnp.float32)
        total = jnp.einsum('thf,thd->hfd', phi_key, value_blk.reshape(TOK_DEV, HEADS, HD).astype(jnp.float32))
        return ((far_state + prev_total, total, key_blk, value_blk), result)
    zero_state = jnp.zeros((HEADS, BUCKETS * BUCKETS, HD), jnp.float32)
    zero_rows = jnp.zeros((TOK_DEV, HEADS * HD), jnp.bfloat16)
    init = (zero_state, zero_state, zero_rows, zero_rows)
    final, results = lax.scan(advance, init, (query_b, key_b, value_b))
    return results.reshape(length, HEADS * HD)
```

```python
import jax
import jax.numpy as jnp
from jax import lax
from jax.experimental import pallas as pl
from jax.experimental.pallas import tpu as pltpu
from jax.sharding import PartitionSpec as P

HD = 128
BUCKETS = 16
SHIFTS = BUCKETS // 2 + 1
FEATURES = SHIFTS * BUCKETS
FACTOR4 = (0.75 * (BUCKETS / HD) ** 0.5) ** 4
EPS = 1e-06
BF16 = jnp.bfloat16
F32 = jnp.float32


def dot_nt(a, b):
    return lax.dot_general(a, b, (((1,), (1,)), ((), ())), preferred_element_type=F32)


def dot_nn(a, b):
    return lax.dot_general(a, b, (((1,), (0,)), ((), ())), preferred_element_type=F32)


def sketch_rows(buckets, hash_row, sign_row, weight=1.0):
    signs = (2 * sign_row - 1).astype(F32) * weight
    return jnp.where(hash_row == buckets, signs, 0.0).astype(BF16)


def head_cols(head):
    return pl.ds(head * HD, HD)


def state_kernel(hash_ref, sign_ref, key_ref, value_ref, total_ref):
    heads = key_ref.shape[1] // HD
    row = lax.broadcasted_iota(jnp.int32, (FEATURES, HD), 0)
    buckets = (row + row // BUCKETS) % BUCKETS
    sketch = jnp.concatenate(
        [
            sketch_rows(buckets, hash_ref[level : level + 1, :], sign_ref[level : level + 1, :])
            for level in range(2)
        ],
        0,
    )
    for head in range(heads):
        both = dot_nt(sketch, key_ref[:, head_cols(head)])
        level = both[:FEATURES] * both[FEATURES:]
        base = level[:BUCKETS] * FACTOR4
        phi = jnp.concatenate(
            [base * level[d * BUCKETS : (d + 1) * BUCKETS] for d in range(SHIFTS)], 0
        ).astype(BF16)
        total = dot_nn(phi, value_ref[:, head_cols(head)])
        total_ref[head] = total.astype(total_ref.dtype)


def quartic(scores):
    squared = scores * scores * (1.0 / HD)
    return squared * squared


def own_kernel(query_ref, key_ref, value_ref, near_ref):
    rows = query_ref.shape[0]
    heads = query_ref.shape[1] // HD
    half = rows // 2
    rows_index = lax.broadcasted_iota(jnp.int32, (half, half), 0)
    cols_index = lax.broadcasted_iota(jnp.int32, (half, half), 1)
    allowed = cols_index <= rows_index
    for head in range(heads):
        cols = head_cols(head)
        key_top, key_low = key_ref[:half, cols], key_ref[half:, cols]
        value_top, value_low = value_ref[:half, cols], value_ref[half:, cols]
        top = jnp.where(allowed, quartic(dot_nt(query_ref[:half, cols], key_top)), 0.0)
        near_ref[:half, cols] = dot_nn(top.astype(BF16), value_top)
        query_low = query_ref[half:, cols]
        left = quartic(dot_nt(query_low, key_top))
        right = jnp.where(allowed, quartic(dot_nt(query_low, key_low)), 0.0)
        near_ref[half:, cols] = dot_nn(left.astype(BF16), value_top) + dot_nn(
            right.astype(BF16), value_low
        )


def before_kernel(query_ref, key_ref, value_ref, own_ref, near_ref):
    heads = query_ref.shape[1] // HD
    for head in range(heads):
        cols = head_cols(head)
        weights = quartic(dot_nt(query_ref[:, cols], key_ref[:, cols])).astype(BF16)
        near_ref[:, cols] = own_ref[:, cols] + dot_nn(weights, value_ref[:, cols])


def far_kernel(hash_ref, sign_ref, query_ref, far_ref, near_ref, gain_ref, out_ref):
    heads = query_ref.shape[1] // HD
    row = lax.broadcasted_iota(jnp.int32, (HD, HD), 0)
    base_bucket = row % BUCKETS
    shift = row // BUCKETS
    weight = jnp.where(shift == 0, 1.0, 2.0)
    pieces = []
    for level in range(2):
        hash_row = hash_ref[level : level + 1, :]
        sign_row = sign_ref[level : level + 1, :]
        pieces.append(sketch_rows(base_bucket, hash_row, sign_row))
        pieces.append(
            sketch_rows(
                (base_bucket + shift) % BUCKETS, hash_row, sign_row, weight if level == 0 else 1.0
            )
        )
    sketch = jnp.concatenate(pieces, 0)
    for head in range(heads):
        cols = head_cols(head)
        both = dot_nt(query_ref[:, cols], sketch)
        first = both[:, :HD] * both[:, 2 * HD : 3 * HD] * FACTOR4
        second = both[:, HD : 2 * HD] * both[:, 3 * HD :]
        opposite = second[:, :BUCKETS]
        opposite = jnp.concatenate(
            [opposite[:, BUCKETS // 2 :], opposite[:, : BUCKETS // 2]], 1
        )
        last = first[:, :BUCKETS] * opposite
        phi = jnp.concatenate([(first * second).astype(BF16), last.astype(BF16)], 1)
        mixed = near_ref[:, cols] + dot_nn(phi, far_ref[head])
        mean_square = jnp.mean(mixed * mixed, axis=-1, keepdims=True)
        out_ref[:, cols] = (
            mixed * lax.rsqrt(mean_square + EPS) * gain_ref[:, cols]
        ).astype(BF16)


def kernel_call(body, out_shape, *args):
    return pl.pallas_call(
        body,
        out_shape=out_shape,
        compiler_params=pltpu.CompilerParams(vmem_limit_bytes=48 * 1024 * 1024),
        name=body.__name__,
    )(*args)


def from_behind(block, axis, distance):
    devices = range(lax.axis_size(axis))
    route = [(i - distance, i) for i in devices if i - distance in devices]
    return lax.ppermute(block, axis, route)


def local(queries, keys, values, out_gain, hash_ids, sign_ids):
    rows, width = queries.shape
    heads = width // HD
    devices = lax.axis_size("seq")
    near_shape = jax.ShapeDtypeStruct((rows, width), F32)
    state_shape = jax.ShapeDtypeStruct((heads, FEATURES, HD), BF16)

    key_prev, value_prev = from_behind((keys, values), "seq", 1)
    total = kernel_call(state_kernel, state_shape, hash_ids, sign_ids, keys, values)
    flat = total.reshape(devices, -1, HD)
    received = lax.all_to_all(flat, "seq", split_axis=0, concat_axis=0, tiled=True)
    running = jnp.cumsum(received.astype(F32), axis=0)
    exclusive = jnp.concatenate(
        [jnp.zeros((2,) + running.shape[1:], F32), running[:-2]], axis=0
    ).astype(BF16)
    gathered = lax.all_to_all(exclusive, "seq", split_axis=0, concat_axis=0, tiled=True)
    far = gathered.reshape(heads, FEATURES, HD)

    near = kernel_call(own_kernel, near_shape, queries, keys, values)
    near = kernel_call(before_kernel, near_shape, queries, key_prev, value_prev, near)
    return kernel_call(
        far_kernel,
        jax.ShapeDtypeStruct((rows, width), BF16),
        hash_ids,
        sign_ids,
        queries,
        far,
        near,
        out_gain.reshape(1, width),
    )


def solution(mesh):
    in_specs = (
        P(("grp", "seq"), "head"),
        P(("grp", "seq"), "head"),
        P(("grp", "seq"), "head"),
        P("head"),
        P(),
        P(),
    )
    out_specs = P(("grp", "seq"), "head")
    return jax.shard_map(local, mesh=mesh, in_specs=in_specs, out_specs=out_specs, check_vma=False)
```

```python
import jax
import jax.numpy as jnp
from jax import lax
from jax.experimental import pallas as pl
from jax.experimental.pallas import tpu as pltpu
from jax.sharding import PartitionSpec as P


HD = 128
BUCKETS = 16
SHIFTS = BUCKETS // 2 + 1
FEATURES = SHIFTS * BUCKETS
FACTOR4 = (0.75 * (BUCKETS / HD) ** 0.5) ** 4
FACTOR2 = (0.75 * (BUCKETS / HD) ** 0.5) ** 2
EPS = 1e-06
CORES = 2
PLANE = 4
BF16 = jnp.bfloat16
F32 = jnp.float32


def dot_nt(a, b):
    return lax.dot_general(a, b, (((1,), (1,)), ((), ())), preferred_element_type=F32)


def dot_nn(a, b):
    return lax.dot_general(a, b, (((1,), (0,)), ((), ())), preferred_element_type=F32)


def sketch_rows(buckets, hash_row, sign_row, weight=1.0):
    signs = (2 * sign_row - 1).astype(F32) * weight
    return jnp.where(hash_row == buckets, signs, 0.0).astype(BF16)


def head_cols(head):
    return pl.ds(head * HD, HD)


def place():
    index = lax.axis_index("seq")
    return index % CORES, (index // CORES) % PLANE


def head_of(core, quarter, inner, per_piece):
    return (core * PLANE + quarter) * per_piece + inner


def cols_of(head):
    return pl.ds(pl.multiple_of(head * HD, HD), HD)


def state_kernel(hash_ref, sign_ref, key_ref, value_ref, keep_ref, send_ref):
    core, chip = place()
    per_piece = keep_ref.shape[1]
    row = lax.broadcasted_iota(jnp.int32, (FEATURES, HD), 0)
    buckets = (row + row // BUCKETS) % BUCKETS
    sketch = jnp.concatenate(
        [
            sketch_rows(buckets, hash_ref[level : level + 1, :], sign_ref[level : level + 1, :])
            for level in range(2)
        ],
        0,
    )
    for side, total_ref in ((1 - core, send_ref), (core, keep_ref)):
        for piece in range(PLANE):
            for inner in range(per_piece):
                cols = cols_of(head_of(side, chip ^ piece, inner, per_piece))
                both = dot_nt(sketch, key_ref[:, cols])
                level = both[:FEATURES] * both[FEATURES:]
                base = level[:BUCKETS] * FACTOR4
                phi = jnp.concatenate(
                    [base * level[d * BUCKETS : (d + 1) * BUCKETS] for d in range(SHIFTS)], 0
                ).astype(BF16)
                total_ref[piece, inner] = dot_nn(phi, value_ref[:, cols])


def quartic(scores):
    squared = scores * scores * (1.0 / HD)
    return squared * squared


def own_kernel(query_ref, key_ref, value_ref, near_ref):
    rows = query_ref.shape[0]
    heads = query_ref.shape[1] // HD
    half = rows // 2
    rows_index = lax.broadcasted_iota(jnp.int32, (half, half), 0)
    cols_index = lax.broadcasted_iota(jnp.int32, (half, half), 1)
    allowed = cols_index <= rows_index
    for head in range(heads):
        cols = head_cols(head)
        key_top, key_low = key_ref[:half, cols], key_ref[half:, cols]
        value_top, value_low = value_ref[:half, cols], value_ref[half:, cols]
        top = jnp.where(allowed, quartic(dot_nt(query_ref[:half, cols], key_top)), 0.0)
        near_ref[:half, cols] = dot_nn(top.astype(BF16), value_top)
        query_low = query_ref[half:, cols]
        left = quartic(dot_nt(query_low, key_top))
        right = jnp.where(allowed, quartic(dot_nt(query_low, key_low)), 0.0)
        near_ref[half:, cols] = dot_nn(left.astype(BF16), value_top) + dot_nn(
            right.astype(BF16), value_low
        )


def split(x):
    high = x.astype(BF16)
    low = (x - high.astype(F32)).astype(BF16)
    return high, low


def before_kernel(hash_ref, sign_ref, query_ref, key_ref, value_ref, own_ref, near_ref):
    core, _ = place()
    even = jnp.where(core == 0, 1.0, 0.0)
    heads = query_ref.shape[1] // HD
    row = lax.broadcasted_iota(jnp.int32, (BUCKETS, HD), 0)
    sketch = jnp.concatenate(
        [
            sketch_rows(row, hash_ref[level : level + 1, :], sign_ref[level : level + 1, :])
            for level in range(2)
        ],
        0,
    )
    for head in range(heads):
        cols = head_cols(head)
        query, key = query_ref[:, cols], key_ref[:, cols]
        query_both = dot_nt(sketch, query)
        key_both = dot_nt(sketch, key)
        query_high, query_low = split(
            query_both[:BUCKETS] * query_both[BUCKETS:] * (even * FACTOR2)
        )
        key_high, key_low = split(key_both[:BUCKETS] * key_both[BUCKETS:] * FACTOR2)
        query_parts = jnp.concatenate([query_high, query_high, query_low], 0)
        key_parts = jnp.concatenate([key_high, key_low, key_high], 0)
        sketched = lax.dot_general(
            query_parts, key_parts, (((0,), (0,)), ((), ())), preferred_element_type=F32
        )
        weights = quartic(dot_nt(query, key)) - sketched * sketched
        near_ref[:, cols] = own_ref[:, cols] + dot_nn(weights.astype(BF16), value_ref[:, cols])


def query_kernel(hash_ref, sign_ref, query_ref, phi_ref):
    heads = query_ref.shape[1] // HD
    row = lax.broadcasted_iota(jnp.int32, (HD, HD), 0)
    base_bucket = row % BUCKETS
    shift = row // BUCKETS
    weight = jnp.where(shift == 0, 1.0, 2.0)
    pieces = []
    for level in range(2):
        hash_row = hash_ref[level : level + 1, :]
        sign_row = sign_ref[level : level + 1, :]
        pieces.append(sketch_rows(base_bucket, hash_row, sign_row))
        pieces.append(
            sketch_rows(
                (base_bucket + shift) % BUCKETS, hash_row, sign_row, weight if level == 0 else 1.0
            )
        )
    sketch = jnp.concatenate(pieces, 0)
    for head in range(heads):
        both = dot_nt(query_ref[:, head_cols(head)], sketch)
        first = both[:, :HD] * both[:, 2 * HD : 3 * HD] * FACTOR4
        second = both[:, HD : 2 * HD] * both[:, 3 * HD :]
        opposite = second[:, :BUCKETS]
        opposite = jnp.concatenate(
            [opposite[:, BUCKETS // 2 :], opposite[:, : BUCKETS // 2]], 1
        )
        last = first[:, :BUCKETS] * opposite
        phi_ref[head, :, :HD] = (first * second).astype(BF16)
        phi_ref[head, :, HD:] = last.astype(BF16)


def far_kernel(phi_ref, mine_ref, theirs_ref, near_ref, gain_ref, out_ref):
    core, chip = place()
    per_piece = mine_ref.shape[1]
    for side, far_ref in ((core, mine_ref), (1 - core, theirs_ref)):
        for piece in range(PLANE):
            for inner in range(per_piece):
                head = head_of(side, chip ^ piece, inner, per_piece)
                cols = cols_of(head)
                mixed = near_ref[:, cols] + dot_nn(phi_ref[head], far_ref[piece, inner])
                mean_square = jnp.mean(mixed * mixed, axis=-1, keepdims=True)
                out_ref[:, cols] = (
                    mixed * lax.rsqrt(mean_square + EPS) * gain_ref[:, cols]
                ).astype(BF16)


def kernel_call(body, out_shape, *args):
    return pl.pallas_call(
        body,
        out_shape=out_shape,
        compiler_params=pltpu.CompilerParams(vmem_limit_bytes=16 * 1024 * 1024),
    )(*args)


def from_behind(block, axis, distance):
    devices = range(lax.axis_size(axis))
    route = [(i - distance, i) for i in devices if i - distance in devices]
    return lax.ppermute(block, axis, route)


def swap(block, mask):
    route = [(i, i ^ mask) for i in range(lax.axis_size("seq"))]
    return lax.ppermute(block, "seq", route)


def earlier_chips(keep, send):
    devices = lax.axis_size("seq")
    index = lax.axis_index("seq")
    chip = (index // CORES) % PLANE
    summed = keep + swap(send, 1)
    shares = [summed[0]] + [
        swap(summed[m].astype(BF16), CORES * m).astype(F32) for m in range(1, PLANE)
    ]
    total = shares[0] + shares[1] + shares[2] + shares[3]
    earlier = jnp.zeros_like(total)
    mask = CORES * PLANE
    while mask < devices:
        got = swap(total.astype(BF16), mask).astype(F32)
        earlier = earlier + jnp.where((index & mask) != 0, got, 0.0)
        total = total + got
        mask *= 2
    prefixes = []
    for m in range(PLANE):
        prefix = earlier
        for other in range(PLANE):
            if other != m:
                prefix = prefix + jnp.where((chip ^ other) < (chip ^ m), shares[other], 0.0)
        prefixes.append(prefix.astype(BF16))
    mine = jnp.stack([prefixes[0]] + [swap(prefixes[m], CORES * m) for m in range(1, PLANE)], 0)
    return mine, swap(mine, 1)


def block_program(queries, keys, values, out_gain, hash_ids, sign_ids):
    rows, width = queries.shape
    heads = width // HD
    near_shape = jax.ShapeDtypeStruct((rows, width), F32)
    half_shape = jax.ShapeDtypeStruct((PLANE, heads // (CORES * PLANE), FEATURES, HD), F32)

    key_prev = from_behind(keys, "seq", 1)
    value_prev = from_behind(values, "seq", 1)
    keep, send = kernel_call(state_kernel, (half_shape, half_shape), hash_ids, sign_ids, keys, values)
    mine, theirs = earlier_chips(keep, send)
    near = kernel_call(own_kernel, near_shape, queries, keys, values)
    phi = kernel_call(
        query_kernel,
        jax.ShapeDtypeStruct((heads, rows, FEATURES), BF16),
        hash_ids,
        sign_ids,
        queries,
    )
    near = kernel_call(
        before_kernel, near_shape, hash_ids, sign_ids, queries, key_prev, value_prev, near
    )
    return kernel_call(
        far_kernel,
        jax.ShapeDtypeStruct((rows, width), BF16),
        phi,
        mine,
        theirs,
        near,
        out_gain.reshape(1, width),
    )


def solution(mesh):
    in_specs = (
        P(("grp", "seq"), "head"),
        P(("grp", "seq"), "head"),
        P(("grp", "seq"), "head"),
        P("head"),
        P(),
        P(),
    )
    out_specs = P(("grp", "seq"), "head")
    return jax.shard_map(
        block_program, mesh=mesh, in_specs=in_specs, out_specs=out_specs, check_vma=False
    )
```

```python
import functools

import jax
import jax.numpy as jnp
from jax import lax
from jax.experimental import pallas as pl
from jax.experimental.pallas import tpu as pltpu
from jax.sharding import PartitionSpec as P


HD = 128
BUCKETS = 16
SHIFTS = BUCKETS // 2 + 1
FEATURES = SHIFTS * BUCKETS
FACTOR4 = (0.75 * (BUCKETS / HD) ** 0.5) ** 4
FACTOR2 = (0.75 * (BUCKETS / HD) ** 0.5) ** 2
EPS = 1e-06
CORES = 2
PLANE = 4
CHUNKS = 4
BF16 = jnp.bfloat16
F32 = jnp.float32
VMEM_LIMIT = 12 * 1024 * 1024
IN_HBM = pl.BlockSpec(memory_space=pltpu.HBM)


def dot_nt(a, b):
    return lax.dot_general(a, b, (((1,), (1,)), ((), ())), preferred_element_type=F32)


def dot_nn(a, b):
    return lax.dot_general(a, b, (((1,), (0,)), ((), ())), preferred_element_type=F32)


def dot_tn(a, b):
    return lax.dot_general(a, b, (((0,), (0,)), ((), ())), preferred_element_type=F32)


def sketch_rows(buckets, hash_row, sign_row, weight=1.0):
    signs = (2 * sign_row - 1).astype(F32) * weight
    return jnp.where(hash_row == buckets, signs, 0.0).astype(BF16)


def head_cols(head):
    return pl.ds(head * HD, HD)


def place():
    index = lax.axis_index("seq")
    return index % CORES, (index // CORES) % PLANE


def side_of(half):
    core, _ = place()
    return 1 - core if half == 0 else core


def dynamic_cols(start, width):
    return pl.ds(pl.multiple_of(start, HD), width)


def quartic(scores):
    squared = scores * scores * (1.0 / HD)
    return squared * squared


def state_kernel(
    hash_hbm,
    sign_hbm,
    query_hbm,
    key_hbm,
    value_hbm,
    send_ref,
    keep_ref,
    hash_ref,
    sign_ref,
    query_0_ref,
    query_1_ref,
    key_0_ref,
    key_1_ref,
    value_0_ref,
    value_1_ref,
    sems,
):
    _, chip = place()
    per_piece = keep_ref.shape[1]
    half_width = key_0_ref.shape[1]
    half_heads = half_width // HD
    chunk_heads = max(half_heads // CHUNKS, 1)
    chunk = chunk_heads * HD
    chunks = half_heads // chunk_heads
    copies = [
        pltpu.make_async_copy(hash_hbm, hash_ref, sems.at[0]),
        pltpu.make_async_copy(sign_hbm, sign_ref, sems.at[1]),
    ]
    halves = ((key_0_ref, value_0_ref), (key_1_ref, value_1_ref))
    for half, refs in enumerate(halves):
        for part in range(chunks):
            cols = dynamic_cols(side_of(half) * half_width + part * chunk, chunk)
            inner = pl.ds(part * chunk, chunk)
            for hbm, ref in zip((key_hbm, value_hbm), refs):
                copies.append(
                    pltpu.make_async_copy(hbm.at[:, cols], ref.at[:, inner], sems.at[len(copies)])
                )
    for half, ref in enumerate((query_0_ref, query_1_ref)):
        cols = dynamic_cols(side_of(half) * half_width, half_width)
        copies.append(pltpu.make_async_copy(query_hbm.at[:, cols], ref, sems.at[len(copies)]))
    for copy in copies:
        copy.start()
    copies[0].wait()
    copies[1].wait()
    row = lax.broadcasted_iota(jnp.int32, (FEATURES, HD), 0)
    buckets = (row + row // BUCKETS) % BUCKETS
    sketch = jnp.concatenate(
        [
            sketch_rows(buckets, hash_ref[level : level + 1, :], sign_ref[level : level + 1, :])
            for level in range(2)
        ],
        0,
    )
    for half, (key_ref, value_ref) in enumerate(halves):
        total_ref = (send_ref, keep_ref)[half]
        for head in range(half_heads):
            if head % chunk_heads == 0:
                first = 2 + 2 * (half * chunks + head // chunk_heads)
                copies[first].wait()
                copies[first + 1].wait()
            cols = head_cols(head)
            both = dot_nt(sketch, key_ref[:, cols])
            level = both[:FEATURES] * both[FEATURES:]
            base = level[:BUCKETS] * FACTOR4
            phi = jnp.concatenate(
                [base * level[d * BUCKETS : (d + 1) * BUCKETS] for d in range(SHIFTS)], 0
            ).astype(BF16)
            total_ref[(head // per_piece) ^ chip, head % per_piece] = dot_nn(
                phi, value_ref[:, cols]
            )
    copies[-2].wait()
    copies[-1].wait()


def query_kernel(hash_ref, sign_ref, query_0_ref, query_1_ref, phi_ref):
    half_heads = query_0_ref.shape[1] // HD
    row = lax.broadcasted_iota(jnp.int32, (HD, HD), 0)
    base_bucket = row % BUCKETS
    shift = row // BUCKETS
    weight = jnp.where(shift == 0, 1.0, 2.0)
    pieces = []
    for level in range(2):
        hash_row = hash_ref[level : level + 1, :]
        sign_row = sign_ref[level : level + 1, :]
        pieces.append(sketch_rows(base_bucket, hash_row, sign_row))
        pieces.append(
            sketch_rows(
                (base_bucket + shift) % BUCKETS, hash_row, sign_row, weight if level == 0 else 1.0
            )
        )
    sketch = jnp.concatenate(pieces, 0)
    for half, query_ref in enumerate((query_0_ref, query_1_ref)):
        for head in range(half_heads):
            both = dot_nt(query_ref[:, head_cols(head)], sketch)
            first = both[:, :HD] * both[:, 2 * HD : 3 * HD] * FACTOR4
            second = both[:, HD : 2 * HD] * both[:, 3 * HD :]
            opposite = second[:, :BUCKETS]
            opposite = jnp.concatenate(
                [opposite[:, BUCKETS // 2 :], opposite[:, : BUCKETS // 2]], 1
            )
            last = first[:, :BUCKETS] * opposite
            phi_ref[half * half_heads + head, :, :HD] = (first * second).astype(BF16)
            phi_ref[half * half_heads + head, :, HD:] = last.astype(BF16)


def own_kernel(query_ref, key_ref, value_ref, near_ref):
    rows = query_ref.shape[0]
    half = rows // 2
    allowed = lax.broadcasted_iota(jnp.int32, (rows, half), 1) <= lax.broadcasted_iota(
        jnp.int32, (rows, half), 0
    )
    for head in range(query_ref.shape[1] // HD):
        cols = head_cols(head)
        query = query_ref[:, cols]
        left = jnp.where(allowed, quartic(dot_nt(query, key_ref[:half, cols])), 0.0)
        right = jnp.where(
            allowed[:half], quartic(dot_nt(query[half:], key_ref[half:, cols])), 0.0
        )
        near = dot_nn(left.astype(BF16), value_ref[:half, cols])
        near_ref[:half, cols] = near[:half]
        near_ref[half:, cols] = near[half:] + dot_nn(right.astype(BF16), value_ref[half:, cols])


def split(x):
    high = x.astype(BF16)
    low = (x - high.astype(F32)).astype(BF16)
    return high, low


def weights_kernel(half, hash_ref, sign_ref, query_ref, key_ref, weight_ref):
    core, _ = place()
    even = jnp.where(core == 0, 1.0, 0.0)
    half_width = query_ref.shape[1]
    row = lax.broadcasted_iota(jnp.int32, (BUCKETS, HD), 0)
    sketch = jnp.concatenate(
        [
            sketch_rows(row, hash_ref[level : level + 1, :], sign_ref[level : level + 1, :])
            for level in range(2)
        ],
        0,
    )
    for head in range(half_width // HD):
        query = query_ref[:, head_cols(head)]
        key = key_ref[:, dynamic_cols(side_of(half) * half_width + head * HD, HD)]
        query_both = dot_nt(sketch, query)
        key_both = dot_nt(sketch, key)
        query_high, query_low = split(
            query_both[:BUCKETS] * query_both[BUCKETS:] * (even * FACTOR2)
        )
        key_high, key_low = split(key_both[:BUCKETS] * key_both[BUCKETS:] * FACTOR2)
        query_parts = jnp.concatenate([query_high, query_high, query_low], 0)
        key_parts = jnp.concatenate([key_high, key_low, key_high], 0)
        sketched = dot_tn(query_parts, key_parts)
        weights = quartic(dot_nt(query, key)) - sketched * sketched
        weight_ref[head] = weights.astype(BF16)


def values_kernel(weight_ref, value_ref, own_ref, near_ref):
    for head in range(weight_ref.shape[0]):
        cols = head_cols(head)
        near_ref[:, cols] = own_ref[:, cols] + dot_nn(weight_ref[head], value_ref[:, cols])


def far_kernel(
    phi_ref, theirs_ref, mine_ref, near_0_ref, near_1_ref, gain_ref, out_hbm, out_ref, sems
):
    _, chip = place()
    per_piece = mine_ref.shape[1]
    half_width = near_0_ref.shape[1]
    half_heads = half_width // HD
    width = per_piece * HD
    copies = []
    for half, (far_ref, near_ref) in enumerate(
        ((theirs_ref, near_0_ref), (mine_ref, near_1_ref))
    ):
        for piece in range(PLANE):
            slot = half * PLANE + piece
            start = side_of(half) * half_width + (chip ^ piece) * width
            for inner in range(per_piece):
                head = (chip ^ piece) * per_piece + inner
                mixed = near_ref[:, dynamic_cols(head * HD, HD)] + dot_nn(
                    phi_ref[half * half_heads + head], far_ref[piece, inner]
                )
                mean_square = jnp.mean(mixed * mixed, axis=-1, keepdims=True)
                gain = gain_ref[:, dynamic_cols(start + inner * HD, HD)]
                out_ref[slot, :, head_cols(inner)] = (
                    mixed * lax.rsqrt(mean_square + EPS) * gain
                ).astype(BF16)
            copies.append(
                pltpu.make_async_copy(
                    out_ref.at[slot], out_hbm.at[:, dynamic_cols(start, width)], sems.at[slot]
                )
            )
            copies[-1].start()
    for copy in copies:
        copy.wait()


def kernel_call(body, out_shape, *args, space=pltpu.VMEM, **options):
    return pl.pallas_call(
        body,
        out_shape=out_shape,
        compiler_params=pltpu.CompilerParams(vmem_limit_bytes=VMEM_LIMIT),
        **options,
    )(*[pltpu.with_memory_space_constraint(arg, space) for arg in args])


def from_behind(block, axis, distance):
    devices = range(lax.axis_size(axis))
    route = [(i - distance, i) for i in devices if i - distance in devices]
    return lax.ppermute(block, axis, route)


def swap(block, mask):
    route = [(i, i ^ mask) for i in range(lax.axis_size("seq"))]
    return lax.ppermute(block, "seq", route)


def chip_sum_kernel(keep_ref, got_ref, own_ref, *share_refs):
    own_ref[...] = keep_ref[0] + got_ref[0]
    for piece, share_ref in enumerate(share_refs, 1):
        share_ref[...] = (keep_ref[piece] + got_ref[piece]).astype(BF16)


def plane_sum_kernel(own_ref, *refs):
    share_refs, (total_ref, sent_ref) = refs[:-2], refs[-2:]
    total = own_ref[...]
    for share_ref in share_refs:
        total = total + share_ref[...].astype(F32)
    total_ref[...] = total
    sent_ref[...] = total.astype(BF16)


def later_half(mask):
    return (lax.axis_index("seq") // mask) % 2


def first_across_kernel(mask, total_ref, got_ref, earlier_ref, more_ref, sent_ref):
    got = got_ref[...].astype(F32)
    earlier_ref[...] = jnp.where(later_half(mask) == 1, got, 0.0)
    total = total_ref[...] + got
    more_ref[...] = total
    sent_ref[...] = total.astype(BF16)


def next_across_kernel(mask, earlier_before_ref, total_ref, got_ref, earlier_ref, more_ref, sent_ref):
    got = got_ref[...].astype(F32)
    earlier_ref[...] = earlier_before_ref[...] + jnp.where(later_half(mask) == 1, got, 0.0)
    total = total_ref[...] + got
    more_ref[...] = total
    sent_ref[...] = total.astype(BF16)


def prefix_kernel(mask, earlier_ref, got_ref, *refs):
    _, chip = place()
    share_refs, prefix_refs = refs[:PLANE], refs[PLANE:]
    earlier = earlier_ref[...] + jnp.where(later_half(mask) == 1, got_ref[...].astype(F32), 0.0)
    shares = [share_ref[...].astype(F32) for share_ref in share_refs]
    for piece, prefix_ref in enumerate(prefix_refs):
        prefix = earlier
        for other in range(PLANE):
            if other != piece:
                ahead = (chip ^ other) < (chip ^ piece)
                prefix = prefix + jnp.where(ahead, shares[other], 0.0)
        prefix_ref[...] = prefix.astype(BF16)


def stack_kernel(*refs):
    piece_refs, all_ref = refs[:-1], refs[-1]
    for piece, piece_ref in enumerate(piece_refs):
        all_ref[piece] = piece_ref[...]


def earlier_chips(keep, send):
    devices = lax.axis_size("seq")
    dims = keep.shape[1:]
    wide, narrow = pltpu.VMEM(dims, F32), pltpu.VMEM(dims, BF16)
    own, *sent = kernel_call(
        chip_sum_kernel, (wide,) + (narrow,) * (PLANE - 1), keep, swap(send, 1)
    )
    shares = [own] + [swap(block, CORES * m) for m, block in enumerate(sent, 1)]
    total, block = kernel_call(plane_sum_kernel, (wide, narrow), *shares)
    mask = CORES * PLANE
    got = swap(block, mask)
    earlier, total, block = kernel_call(
        functools.partial(first_across_kernel, mask), (wide, wide, narrow), total, got
    )
    mask *= 2
    got = swap(block, mask)
    while mask * 2 < devices:
        earlier, total, block = kernel_call(
            functools.partial(next_across_kernel, mask), (wide, wide, narrow), earlier, total, got
        )
        mask *= 2
        got = swap(block, mask)
    prefixes = kernel_call(
        functools.partial(prefix_kernel, mask), (narrow,) * PLANE, earlier, got, *shares
    )
    mine = kernel_call(
        stack_kernel,
        pltpu.VMEM((PLANE,) + dims, BF16),
        prefixes[0],
        *[swap(prefixes[m], CORES * m) for m in range(1, PLANE)],
    )
    return mine, swap(mine, 1)


def block_program(queries, keys, values, out_gain, hash_ids, sign_ids):
    rows, width = queries.shape
    heads = width // HD
    half_heads = heads // 2
    half_state = pltpu.VMEM((PLANE, heads // (CORES * PLANE), FEATURES, HD), F32)
    half_rows = pltpu.VMEM((rows, width // 2), BF16)
    half_near = pltpu.VMEM((rows, width // 2), F32)
    id_shape = pltpu.VMEM(hash_ids.shape, hash_ids.dtype)

    key_prev = from_behind(keys, "seq", 1)
    send, keep, hash_near, sign_near, query_0, query_1, key_0, key_1, value_0, value_1 = kernel_call(
        state_kernel,
        (half_state, half_state, id_shape, id_shape) + (half_rows,) * 6,
        hash_ids,
        sign_ids,
        queries,
        keys,
        values,
        space=pltpu.HBM,
        in_specs=[IN_HBM] * 5,
        scratch_shapes=[pltpu.SemaphoreType.DMA((4 + 4 * CHUNKS,))],
    )
    value_prev_1 = from_behind(value_0, "seq", 1)
    value_prev_0 = from_behind(value_1, "seq", 1)
    mine, theirs = earlier_chips(keep, send)
    phi = kernel_call(
        query_kernel,
        pltpu.VMEM((heads, rows, FEATURES), BF16),
        hash_near,
        sign_near,
        query_0,
        query_1,
    )
    near = []
    for half, query, key, value, value_prev in (
        (0, query_0, key_0, value_0, value_prev_0),
        (1, query_1, key_1, value_1, value_prev_1),
    ):
        own = kernel_call(own_kernel, half_near, query, key, value)
        weights = kernel_call(
            functools.partial(weights_kernel, half),
            pltpu.VMEM((half_heads, rows, rows), BF16),
            hash_near,
            sign_near,
            query,
            key_prev,
        )
        near.append(kernel_call(values_kernel, half_near, weights, value_prev, own))
    return kernel_call(
        far_kernel,
        pltpu.HBM((rows, width), BF16),
        phi,
        theirs,
        mine,
        *near,
        out_gain.reshape(1, width),
        out_specs=IN_HBM,
        scratch_shapes=[
            pltpu.VMEM((CORES * PLANE, rows, width // (CORES * PLANE)), BF16),
            pltpu.SemaphoreType.DMA((CORES * PLANE,)),
        ],
    )


def solution(mesh):
    in_specs = (
        P(("grp", "seq"), "head"),
        P(("grp", "seq"), "head"),
        P(("grp", "seq"), "head"),
        P("head"),
        P(),
        P(),
    )
    out_specs = P(("grp", "seq"), "head")
    return jax.shard_map(
        block_program, mesh=mesh, in_specs=in_specs, out_specs=out_specs, check_vma=False
    )
```

```python
import functools

import jax
import jax.numpy as jnp
from jax import lax
from jax.experimental import pallas as pl
from jax.experimental.pallas import tpu as pltpu
from jax.sharding import PartitionSpec as P


HD = 128
BUCKETS = 16
SHIFTS = BUCKETS // 2 + 1
FEATURES = SHIFTS * BUCKETS
FACTOR4 = (0.75 * (BUCKETS / HD) ** 0.5) ** 4
FACTOR2 = (0.75 * (BUCKETS / HD) ** 0.5) ** 2
EPS = 1e-06
CORES = 2
PLANE = 4
RADIX = 2
CHUNKS = 2
BF16 = jnp.bfloat16
F32 = jnp.float32
VMEM_LIMIT = 12 * 1024 * 1024
IN_HBM = pl.BlockSpec(memory_space=pltpu.HBM)


def dot_nt(a, b):
    return lax.dot_general(a, b, (((1,), (1,)), ((), ())), preferred_element_type=F32)


def dot_nn(a, b):
    return lax.dot_general(a, b, (((1,), (0,)), ((), ())), preferred_element_type=F32)


def dot_tn(a, b):
    return lax.dot_general(a, b, (((0,), (0,)), ((), ())), preferred_element_type=F32)


def sketch_rows(buckets, hash_row, sign_row, weight=1.0):
    signs = (2 * sign_row - 1).astype(F32) * weight
    return jnp.where(hash_row == buckets, signs, 0.0).astype(BF16)


def head_cols(head):
    return pl.ds(head * HD, HD)


def place():
    index = lax.axis_index("seq")
    return index % CORES, (index // CORES) % PLANE


def side_of(half):
    core, _ = place()
    return 1 - core if half == 0 else core


def dynamic_cols(start, width):
    return pl.ds(pl.multiple_of(start, HD), width)


def quartic(scores, factor=1.0 / HD):
    squared = scores * scores * factor
    return squared * squared


def state_kernel(
    hash_hbm,
    sign_hbm,
    query_hbm,
    key_hbm,
    value_hbm,
    send_ref,
    keep_ref,
    hash_ref,
    sign_ref,
    query_0_ref,
    query_1_ref,
    key_0_ref,
    key_1_ref,
    value_0_ref,
    value_1_ref,
    sems,
):
    _, chip = place()
    per_piece = keep_ref.shape[1]
    half_width = key_0_ref.shape[1]
    half_heads = half_width // HD
    chunk_heads = max(half_heads // CHUNKS, 1)
    chunk = chunk_heads * HD
    chunks = half_heads // chunk_heads
    copies = [
        pltpu.make_async_copy(hash_hbm, hash_ref, sems.at[0]),
        pltpu.make_async_copy(sign_hbm, sign_ref, sems.at[1]),
    ]
    halves = ((key_0_ref, value_0_ref), (key_1_ref, value_1_ref))
    for half, refs in enumerate(halves):
        for part in range(chunks):
            cols = dynamic_cols(side_of(half) * half_width + part * chunk, chunk)
            inner = pl.ds(part * chunk, chunk)
            for hbm, ref in zip((key_hbm, value_hbm), refs):
                copies.append(
                    pltpu.make_async_copy(hbm.at[:, cols], ref.at[:, inner], sems.at[len(copies)])
                )
    for half, ref in enumerate((query_0_ref, query_1_ref)):
        cols = dynamic_cols(side_of(half) * half_width, half_width)
        copies.append(pltpu.make_async_copy(query_hbm.at[:, cols], ref, sems.at[len(copies)]))
    for copy in copies:
        copy.start()
    copies[0].wait()
    copies[1].wait()
    row = lax.broadcasted_iota(jnp.int32, (FEATURES, HD), 0)
    buckets = (row + row // BUCKETS) % BUCKETS
    sketch = jnp.concatenate(
        [
            sketch_rows(buckets, hash_ref[level : level + 1, :], sign_ref[level : level + 1, :])
            for level in range(2)
        ],
        0,
    )
    for half, (key_ref, value_ref) in enumerate(halves):
        total_ref = (send_ref, keep_ref)[half]
        for head in range(half_heads):
            if head % chunk_heads == 0:
                first = 2 + 2 * (half * chunks + head // chunk_heads)
                copies[first].wait()
                copies[first + 1].wait()
            cols = head_cols(head)
            both = dot_nt(sketch, key_ref[:, cols])
            level = both[:FEATURES] * both[FEATURES:]
            base = level[:BUCKETS] * FACTOR4
            phi = jnp.concatenate(
                [base * level[d * BUCKETS : (d + 1) * BUCKETS] for d in range(SHIFTS)], 0
            ).astype(BF16)
            total_ref[(head // per_piece) ^ chip, head % per_piece] = dot_nn(
                phi, value_ref[:, cols]
            )
    copies[-2].wait()
    copies[-1].wait()


def query_kernel(hash_ref, sign_ref, query_0_ref, query_1_ref, phi_ref):
    half_heads = query_0_ref.shape[1] // HD
    row = lax.broadcasted_iota(jnp.int32, (HD, HD), 0)
    base_bucket = row % BUCKETS
    shift = row // BUCKETS
    weight = jnp.where(shift == 0, 1.0, 2.0)
    pieces = []
    for level in range(2):
        hash_row = hash_ref[level : level + 1, :]
        sign_row = sign_ref[level : level + 1, :]
        pieces.append(sketch_rows(base_bucket, hash_row, sign_row))
        pieces.append(
            sketch_rows(
                (base_bucket + shift) % BUCKETS, hash_row, sign_row, weight if level == 0 else 1.0
            )
        )
    sketch = jnp.concatenate(pieces, 0)
    for half, query_ref in enumerate((query_0_ref, query_1_ref)):
        for head in range(half_heads):
            both = dot_nt(query_ref[:, head_cols(head)], sketch)
            first = both[:, :HD] * both[:, 2 * HD : 3 * HD] * FACTOR4
            second = both[:, HD : 2 * HD] * both[:, 3 * HD :]
            opposite = second[:, :BUCKETS]
            opposite = jnp.concatenate(
                [opposite[:, BUCKETS // 2 :], opposite[:, : BUCKETS // 2]], 1
            )
            last = first[:, :BUCKETS] * opposite
            phi_ref[half * half_heads + head, :, :HD] = (first * second).astype(BF16)
            phi_ref[half * half_heads + head, :, HD:] = last.astype(BF16)


def own_kernel(query_ref, key_ref, value_ref, near_ref):
    rows = query_ref.shape[0]
    half = rows // 2
    allowed = lax.broadcasted_iota(jnp.int32, (rows, half), 1) <= lax.broadcasted_iota(
        jnp.int32, (rows, half), 0
    )
    for head in range(query_ref.shape[1] // HD):
        cols = head_cols(head)
        query = query_ref[:, cols]
        left = jnp.where(allowed, quartic(dot_nt(query, key_ref[:half, cols])), 0.0)
        right = jnp.where(
            allowed[:half], quartic(dot_nt(query[half:], key_ref[half:, cols])), 0.0
        )
        near = dot_nn(left.astype(BF16), value_ref[:half, cols])
        near_ref[:half, cols] = near[:half]
        near_ref[half:, cols] = near[half:] + dot_nn(right.astype(BF16), value_ref[half:, cols])


def split(x):
    high = x.astype(BF16)
    low = (x - high.astype(F32)).astype(BF16)
    return high, low


def weights_kernel(half, hash_ref, sign_ref, query_ref, key_ref, weight_ref):
    core, _ = place()
    width = query_ref.shape[1]
    heads = width // HD

    def key_of(head):
        return key_ref[:, dynamic_cols(side_of(half) * width + head * HD, HD)]

    @pl.when(core == 1)
    def _():
        for head in range(heads):
            cols = head_cols(head)
            weight_ref[head] = quartic(dot_nt(query_ref[:, cols], key_of(head))).astype(BF16)

    @pl.when(core == 0)
    def _():
        live = jnp.where(lax.axis_index("seq") == 0, 0.0, 1.0)
        row = lax.broadcasted_iota(jnp.int32, (BUCKETS, HD), 0)
        sketch = jnp.concatenate(
            [
                sketch_rows(row, hash_ref[level : level + 1, :], sign_ref[level : level + 1, :])
                for level in range(2)
            ],
            0,
        )
        for head in range(heads):
            cols = head_cols(head)
            query, key = query_ref[:, cols], key_of(head)
            query_both = dot_nt(sketch, query)
            key_both = dot_nt(sketch, key)
            query_high, query_low = split(query_both[:BUCKETS] * query_both[BUCKETS:] * (live * FACTOR2))
            key_high, key_low = split(key_both[:BUCKETS] * key_both[BUCKETS:] * FACTOR2)
            query_parts = jnp.concatenate([query_high, query_high, query_low], 0)
            key_parts = jnp.concatenate([key_high, key_low, key_high], 0)
            sketched = dot_tn(query_parts, key_parts)
            weights = quartic(dot_nt(query, key), live / HD) - sketched * sketched
            weight_ref[head] = weights.astype(BF16)


def values_kernel(weight_ref, value_ref, own_ref, near_ref):
    for head in range(weight_ref.shape[0]):
        cols = head_cols(head)
        near_ref[:, cols] = own_ref[:, cols] + dot_nn(weight_ref[head], value_ref[:, cols])


def far_kernel(
    phi_ref, theirs_ref, mine_ref, near_0_ref, near_1_ref, gain_ref, out_hbm, out_ref, sems
):
    _, chip = place()
    per_piece = mine_ref.shape[1]
    half_width = near_0_ref.shape[1]
    half_heads = half_width // HD
    width = per_piece * HD
    copies = []
    for half, (far_ref, near_ref) in enumerate(
        ((theirs_ref, near_0_ref), (mine_ref, near_1_ref))
    ):
        for piece in range(PLANE):
            slot = half * PLANE + piece
            start = side_of(half) * half_width + (chip ^ piece) * width
            for inner in range(per_piece):
                head = (chip ^ piece) * per_piece + inner
                mixed = near_ref[:, dynamic_cols(head * HD, HD)] + dot_nn(
                    phi_ref[half * half_heads + head], far_ref[piece, inner]
                )
                mean_square = jnp.mean(mixed * mixed, axis=-1, keepdims=True)
                gain = gain_ref[:, dynamic_cols(start + inner * HD, HD)]
                out_ref[slot, :, head_cols(inner)] = (
                    mixed * lax.rsqrt(mean_square + EPS) * gain
                ).astype(BF16)
            copies.append(
                pltpu.make_async_copy(
                    out_ref.at[slot], out_hbm.at[:, dynamic_cols(start, width)], sems.at[slot]
                )
            )
            copies[-1].start()
    for copy in copies:
        copy.wait()


def kernel_call(body, out_shape, *args, space=pltpu.VMEM, **options):
    return pl.pallas_call(
        body,
        out_shape=out_shape,
        compiler_params=pltpu.CompilerParams(vmem_limit_bytes=VMEM_LIMIT),
        **options,
    )(*[pltpu.with_memory_space_constraint(arg, space) for arg in args])


def from_behind(block, closed=False):
    devices = lax.axis_size("seq")
    route = [(i, (i + 1) % devices) for i in range(devices if closed else devices - 1)]
    return lax.ppermute(block, "seq", route)


def swap(block, mask):
    route = [(i, i ^ mask) for i in range(lax.axis_size("seq"))]
    return lax.ppermute(block, "seq", route)


def chip_sum_kernel(keep_ref, got_ref, own_ref, *share_refs):
    own_ref[...] = keep_ref[0] + got_ref[0]
    for piece, share_ref in enumerate(share_refs, 1):
        share_ref[...] = (keep_ref[piece] + got_ref[piece]).astype(BF16)


def plane_sum_kernel(own_ref, *refs):
    share_refs, (total_ref, sent_ref) = refs[:-2], refs[-2:]
    total = own_ref[...]
    for share_ref in share_refs:
        total = total + share_ref[...].astype(F32)
    total_ref[...] = total
    sent_ref[...] = total.astype(BF16)


def sum_of_earlier(unit, got_refs):
    digit = (lax.axis_index("seq") // unit) % (len(got_refs) + 1)
    earlier = 0.0
    for other, got_ref in enumerate(got_refs, 1):
        ahead = (digit ^ other) < digit
        earlier = earlier + jnp.where(ahead, got_ref[...].astype(F32), 0.0)
    return earlier


def across_kernel(unit, known, total_ref, *refs):
    known_refs, got_refs, (earlier_ref, more_ref, sent_ref) = refs[:known], refs[known:-3], refs[-3:]
    earlier = sum_of_earlier(unit, got_refs)
    for known_ref in known_refs:
        earlier = earlier + known_ref[...]
    earlier_ref[...] = earlier
    total = total_ref[...]
    for got_ref in got_refs:
        total = total + got_ref[...].astype(F32)
    more_ref[...] = total
    sent_ref[...] = total.astype(BF16)


def prefix_kernel(unit, known, *refs):
    _, chip = place()
    known_refs, share_refs = refs[:known], refs[known : known + PLANE]
    got_refs, prefix_refs = refs[known + PLANE : -PLANE], refs[-PLANE:]
    earlier = sum_of_earlier(unit, got_refs)
    for known_ref in known_refs:
        earlier = earlier + known_ref[...]
    shares = [share_ref[...].astype(F32) for share_ref in share_refs]
    for piece, prefix_ref in enumerate(prefix_refs):
        prefix = earlier
        for other in range(PLANE):
            if other != piece:
                ahead = (chip ^ other) < (chip ^ piece)
                prefix = prefix + jnp.where(ahead, shares[other], 0.0)
        prefix_ref[...] = prefix.astype(BF16)


def stack_kernel(*refs):
    piece_refs, all_ref = refs[:-1], refs[-1]
    for piece, piece_ref in enumerate(piece_refs):
        all_ref[piece] = piece_ref[...]


def earlier_chips(keep, send):
    devices = lax.axis_size("seq")
    dims = keep.shape[1:]
    wide, narrow = pltpu.VMEM(dims, F32), pltpu.VMEM(dims, BF16)
    own, *sent = kernel_call(
        chip_sum_kernel, (wide,) + (narrow,) * (PLANE - 1), keep, swap(send, 1)
    )
    shares = [own] + [swap(block, CORES * m) for m, block in enumerate(sent, 1)]
    total, block = kernel_call(plane_sum_kernel, (wide, narrow), *shares)
    unit, known = CORES * PLANE, ()
    while True:
        radix = min(RADIX, devices // unit)
        got = [swap(block, unit * m) for m in range(1, radix)]
        if unit * radix >= devices:
            break
        earlier, total, block = kernel_call(
            functools.partial(across_kernel, unit, len(known)),
            (wide, wide, narrow),
            total,
            *known,
            *got,
        )
        unit, known = unit * radix, (earlier,)
    prefixes = kernel_call(
        functools.partial(prefix_kernel, unit, len(known)), (narrow,) * PLANE, *known, *shares, *got
    )
    mine = kernel_call(
        stack_kernel,
        pltpu.VMEM((PLANE,) + dims, BF16),
        prefixes[0],
        *[swap(prefixes[m], CORES * m) for m in range(1, PLANE)],
    )
    return mine, swap(mine, 1)


def block_program(queries, keys, values, out_gain, hash_ids, sign_ids):
    rows, width = queries.shape
    heads = width // HD
    half_heads = heads // 2
    half_state = pltpu.VMEM((PLANE, heads // (CORES * PLANE), FEATURES, HD), F32)
    half_rows = pltpu.VMEM((rows, width // 2), BF16)
    half_near = pltpu.VMEM((rows, width // 2), F32)
    id_shape = pltpu.VMEM(hash_ids.shape, hash_ids.dtype)

    send, keep, hash_near, sign_near, query_0, query_1, key_0, key_1, value_0, value_1 = kernel_call(
        state_kernel,
        (half_state, half_state, id_shape, id_shape) + (half_rows,) * 6,
        hash_ids,
        sign_ids,
        queries,
        keys,
        values,
        space=pltpu.HBM,
        in_specs=[IN_HBM] * 5,
        scratch_shapes=[pltpu.SemaphoreType.DMA((4 + 4 * CHUNKS,))],
    )
    key_prev = from_behind(keys, closed=True)
    value_prev_1 = from_behind(value_0)
    value_prev_0 = from_behind(value_1)
    mine, theirs = earlier_chips(keep, send)
    phi = kernel_call(
        query_kernel,
        pltpu.VMEM((heads, rows, FEATURES), BF16),
        hash_near,
        sign_near,
        query_0,
        query_1,
    )
    near = []
    for half, query, key, value, value_prev in (
        (0, query_0, key_0, value_0, value_prev_0),
        (1, query_1, key_1, value_1, value_prev_1),
    ):
        own = kernel_call(own_kernel, half_near, query, key, value)
        weights = kernel_call(
            functools.partial(weights_kernel, half),
            pltpu.VMEM((half_heads, rows, rows), BF16),
            hash_near,
            sign_near,
            query,
            key_prev,
        )
        near.append(kernel_call(values_kernel, half_near, weights, value_prev, own))
    return kernel_call(
        far_kernel,
        pltpu.HBM((rows, width), BF16),
        phi,
        theirs,
        mine,
        *near,
        out_gain.reshape(1, width),
        out_specs=IN_HBM,
        scratch_shapes=[
            pltpu.VMEM((CORES * PLANE, rows, width // (CORES * PLANE)), BF16),
            pltpu.SemaphoreType.DMA((CORES * PLANE,)),
        ],
    )


def solution(mesh):
    in_specs = (
        P(("grp", "seq"), "head"),
        P(("grp", "seq"), "head"),
        P(("grp", "seq"), "head"),
        P("head"),
        P(),
        P(),
    )
    out_specs = P(("grp", "seq"), "head")
    return jax.shard_map(
        block_program, mesh=mesh, in_specs=in_specs, out_specs=out_specs, check_vma=False
    )
```

```python
import functools

import jax
import jax.numpy as jnp
from jax import lax
from jax.experimental import pallas as pl
from jax.experimental.pallas import tpu as pltpu
from jax.sharding import PartitionSpec as P


HD = 128
BUCKETS = 16
SHIFTS = BUCKETS // 2 + 1
FEATURES = SHIFTS * BUCKETS
FACTOR4 = (0.75 * (BUCKETS / HD) ** 0.5) ** 4
FACTOR2 = (0.75 * (BUCKETS / HD) ** 0.5) ** 2
EPS = 1e-06
CORES = 2
PLANE = 4
RADIX = 4
BF16 = jnp.bfloat16
F32 = jnp.float32
VMEM_LIMIT = 12 * 1024 * 1024
IN_HBM = pl.BlockSpec(memory_space=pltpu.HBM)


def dot_nt(a, b):
    return lax.dot_general(a, b, (((1,), (1,)), ((), ())), preferred_element_type=F32)


def dot_nn(a, b):
    return lax.dot_general(a, b, (((1,), (0,)), ((), ())), preferred_element_type=F32)


def dot_tn(a, b):
    return lax.dot_general(a, b, (((0,), (0,)), ((), ())), preferred_element_type=F32)


def sketch_rows(buckets, hash_row, sign_row, weight=1.0):
    signs = (2 * sign_row - 1).astype(F32) * weight
    return jnp.where(hash_row == buckets, signs, 0.0).astype(BF16)


def head_cols(head):
    return pl.ds(head * HD, HD)


def place():
    index = lax.axis_index("seq")
    return index % CORES, (index // CORES) % PLANE


def side_of(half):
    core, _ = place()
    return 1 - core if half == 0 else core


def dynamic_cols(start, width):
    return pl.ds(pl.multiple_of(start, HD), width)


def quartic(scores, factor=1.0 / HD):
    squared = scores * scores * factor
    return squared * squared


def state_kernel(
    hash_hbm,
    sign_hbm,
    query_hbm,
    key_hbm,
    value_hbm,
    send_ref,
    keep_ref,
    hash_ref,
    sign_ref,
    query_0_ref,
    query_1_ref,
    key_0_ref,
    key_1_ref,
    value_0_ref,
    value_1_ref,
    sems,
):
    _, chip = place()
    per_piece = keep_ref.shape[1]
    half_width = key_0_ref.shape[1]
    half_heads = half_width // HD
    cuts = ((0, max(half_heads // 4, 1), half_heads), (0, half_heads))
    copies = [
        pltpu.make_async_copy(hash_hbm, hash_ref, sems.at[0]),
        pltpu.make_async_copy(sign_hbm, sign_ref, sems.at[1]),
    ]
    halves = ((key_0_ref, value_0_ref), (key_1_ref, value_1_ref))
    arrivals = {}
    for half, refs in enumerate(halves):
        for low, high in zip(cuts[half], cuts[half][1:]):
            arrivals[half, low] = len(copies)
            inner = pl.ds(low * HD, (high - low) * HD)
            cols = dynamic_cols(side_of(half) * half_width + low * HD, (high - low) * HD)
            for hbm, ref in zip((key_hbm, value_hbm), refs):
                copies.append(
                    pltpu.make_async_copy(hbm.at[:, cols], ref.at[:, inner], sems.at[len(copies)])
                )
    for copy in copies:
        copy.start()
    for half, ref in enumerate((query_0_ref, query_1_ref)):
        cols = dynamic_cols(side_of(half) * half_width, half_width)
        copies.append(pltpu.make_async_copy(query_hbm.at[:, cols], ref, sems.at[len(copies)]))
    copies[0].wait()
    copies[1].wait()
    row = lax.broadcasted_iota(jnp.int32, (FEATURES, HD), 0)
    buckets = (row + row // BUCKETS) % BUCKETS
    sketch = jnp.concatenate(
        [
            sketch_rows(buckets, hash_ref[level : level + 1, :], sign_ref[level : level + 1, :])
            for level in range(2)
        ],
        0,
    )
    for half, (key_ref, value_ref) in enumerate(halves):
        total_ref = (send_ref, keep_ref)[half]
        for head in range(half_heads):
            if (half, head) in arrivals:
                first = arrivals[half, head]
                copies[first].wait()
                copies[first + 1].wait()
            if (half, head) == (0, half_heads // 2):
                copies[-2].start()
                copies[-1].start()
            cols = head_cols(head)
            both = dot_nt(sketch, key_ref[:, cols])
            level = both[:FEATURES] * both[FEATURES:]
            base = level[:BUCKETS] * FACTOR4
            phi = jnp.concatenate(
                [base * level[d * BUCKETS : (d + 1) * BUCKETS] for d in range(SHIFTS)], 0
            ).astype(BF16)
            total_ref[(head // per_piece) ^ chip, head % per_piece] = dot_nn(
                phi, value_ref[:, cols]
            )
    copies[-2].wait()
    copies[-1].wait()


def query_kernel(hash_ref, sign_ref, query_0_ref, query_1_ref, phi_ref):
    half_heads = query_0_ref.shape[1] // HD
    row = lax.broadcasted_iota(jnp.int32, (HD, HD), 0)
    base_bucket = row % BUCKETS
    shift = row // BUCKETS
    weight = jnp.where(shift == 0, 1.0, 2.0)
    pieces = []
    for level in range(2):
        hash_row = hash_ref[level : level + 1, :]
        sign_row = sign_ref[level : level + 1, :]
        pieces.append(sketch_rows(base_bucket, hash_row, sign_row))
        pieces.append(
            sketch_rows(
                (base_bucket + shift) % BUCKETS, hash_row, sign_row, weight if level == 0 else 1.0
            )
        )
    sketch = jnp.concatenate(pieces, 0)
    for half, query_ref in enumerate((query_0_ref, query_1_ref)):
        for head in range(half_heads):
            both = dot_nt(query_ref[:, head_cols(head)], sketch)
            first = both[:, :HD] * both[:, 2 * HD : 3 * HD] * FACTOR4
            second = both[:, HD : 2 * HD] * both[:, 3 * HD :]
            opposite = second[:, :BUCKETS]
            opposite = jnp.concatenate(
                [opposite[:, BUCKETS // 2 :], opposite[:, : BUCKETS // 2]], 1
            )
            last = first[:, :BUCKETS] * opposite
            phi_ref[half * half_heads + head, :, :HD] = (first * second).astype(BF16)
            phi_ref[half * half_heads + head, :, HD:] = last.astype(BF16)


def own_kernel(query_ref, key_ref, value_ref, near_ref):
    rows = query_ref.shape[0]
    half = rows // 2
    allowed = lax.broadcasted_iota(jnp.int32, (rows, half), 1) <= lax.broadcasted_iota(
        jnp.int32, (rows, half), 0
    )
    for head in range(query_ref.shape[1] // HD):
        cols = head_cols(head)
        query = query_ref[:, cols]
        left = jnp.where(allowed, quartic(dot_nt(query, key_ref[:half, cols])), 0.0)
        right = jnp.where(
            allowed[:half], quartic(dot_nt(query[half:], key_ref[half:, cols])), 0.0
        )
        near = dot_nn(left.astype(BF16), value_ref[:half, cols])
        near_ref[:half, cols] = near[:half]
        near_ref[half:, cols] = near[half:] + dot_nn(right.astype(BF16), value_ref[half:, cols])


def split(x):
    high = x.astype(BF16)
    low = (x - high.astype(F32)).astype(BF16)
    return high, low


def weights_kernel(half, hash_ref, sign_ref, query_ref, key_ref, weight_ref):
    core, _ = place()
    width = query_ref.shape[1]
    heads = width // HD

    def key_of(head):
        return key_ref[:, dynamic_cols(side_of(half) * width + head * HD, HD)]

    @pl.when(core == 1)
    def _():
        for head in range(heads):
            cols = head_cols(head)
            weight_ref[head] = quartic(dot_nt(query_ref[:, cols], key_of(head))).astype(BF16)

    @pl.when(core == 0)
    def _():
        live = jnp.where(lax.axis_index("seq") == 0, 0.0, 1.0)
        row = lax.broadcasted_iota(jnp.int32, (BUCKETS, HD), 0)
        sketch = jnp.concatenate(
            [
                sketch_rows(row, hash_ref[level : level + 1, :], sign_ref[level : level + 1, :])
                for level in range(2)
            ],
            0,
        )
        for head in range(heads):
            cols = head_cols(head)
            query, key = query_ref[:, cols], key_of(head)
            query_both = dot_nt(sketch, query)
            key_both = dot_nt(sketch, key)
            query_high, query_low = split(query_both[:BUCKETS] * query_both[BUCKETS:] * (live * FACTOR2))
            key_high, key_low = split(key_both[:BUCKETS] * key_both[BUCKETS:] * FACTOR2)
            query_parts = jnp.concatenate([query_high, query_high, query_low], 0)
            key_parts = jnp.concatenate([key_high, key_low, key_high], 0)
            sketched = dot_tn(query_parts, key_parts)
            weights = quartic(dot_nt(query, key), live / HD) - sketched * sketched
            weight_ref[head] = weights.astype(BF16)


def values_kernel(weight_ref, value_ref, own_ref, near_ref):
    for head in range(weight_ref.shape[0]):
        cols = head_cols(head)
        near_ref[:, cols] = own_ref[:, cols] + dot_nn(weight_ref[head], value_ref[:, cols])


def far_kernel(
    phi_ref, theirs_ref, mine_ref, near_0_ref, near_1_ref, gain_ref, out_hbm, out_ref, sems
):
    _, chip = place()
    per_piece = mine_ref.shape[1]
    half_width = near_0_ref.shape[1]
    half_heads = half_width // HD
    width = per_piece * HD
    copies = []
    for half, (far_ref, near_ref) in enumerate(
        ((theirs_ref, near_0_ref), (mine_ref, near_1_ref))
    ):
        for piece in range(PLANE):
            slot = half * PLANE + piece
            start = side_of(half) * half_width + (chip ^ piece) * width
            for inner in range(per_piece):
                head = (chip ^ piece) * per_piece + inner
                mixed = near_ref[:, dynamic_cols(head * HD, HD)] + dot_nn(
                    phi_ref[half * half_heads + head], far_ref[piece, inner]
                )
                mean_square = jnp.mean(mixed * mixed, axis=-1, keepdims=True)
                gain = gain_ref[:, dynamic_cols(start + inner * HD, HD)]
                out_ref[slot, :, head_cols(inner)] = (
                    mixed * lax.rsqrt(mean_square + EPS) * gain
                ).astype(BF16)
            copies.append(
                pltpu.make_async_copy(
                    out_ref.at[slot], out_hbm.at[:, dynamic_cols(start, width)], sems.at[slot]
                )
            )
            copies[-1].start()
    for copy in copies:
        copy.wait()


def kernel_call(body, out_shape, *args, space=pltpu.VMEM, **options):
    return pl.pallas_call(
        body,
        out_shape=out_shape,
        compiler_params=pltpu.CompilerParams(vmem_limit_bytes=VMEM_LIMIT),
        **options,
    )(*[pltpu.with_memory_space_constraint(arg, space) for arg in args])


def from_behind(block, closed=False):
    devices = lax.axis_size("seq")
    route = [(i, (i + 1) % devices) for i in range(devices if closed else devices - 1)]
    return lax.ppermute(block, "seq", route)


def swap(block, mask):
    route = [(i, i ^ mask) for i in range(lax.axis_size("seq"))]
    return lax.ppermute(block, "seq", route)


def chip_sum_kernel(keep_ref, got_ref, own_ref, *share_refs):
    own_ref[...] = keep_ref[0] + got_ref[0]
    for piece, share_ref in enumerate(share_refs, 1):
        share_ref[...] = (keep_ref[piece] + got_ref[piece]).astype(BF16)


def plane_sum_kernel(own_ref, *refs):
    share_refs, total_refs = refs[: PLANE - 1], refs[PLANE - 1 :]
    total = own_ref[...]
    for share_ref in share_refs:
        total = total + share_ref[...].astype(F32)
    for total_ref in total_refs:
        total_ref[...] = total.astype(total_ref.dtype)


def sum_of_earlier(unit, got_refs):
    digit = (lax.axis_index("seq") // unit) % (len(got_refs) + 1)
    earlier = 0.0
    for other, got_ref in enumerate(got_refs, 1):
        ahead = (digit ^ other) < digit
        earlier = earlier + jnp.where(ahead, got_ref[...].astype(F32), 0.0)
    return earlier


def across_kernel(unit, known, radix, total_ref, *refs):
    inputs = known + radix - 1
    known_refs, got_refs, (earlier_ref, *total_refs) = refs[:known], refs[known:inputs], refs[inputs:]
    earlier = sum_of_earlier(unit, got_refs)
    for known_ref in known_refs:
        earlier = earlier + known_ref[...]
    earlier_ref[...] = earlier
    total = total_ref[...]
    for got_ref in got_refs:
        total = total + got_ref[...].astype(F32)
    for more_ref in total_refs:
        more_ref[...] = total.astype(more_ref.dtype)


def prefix_kernel(unit, known, *refs):
    _, chip = place()
    known_refs, share_refs = refs[:known], refs[known : known + PLANE]
    got_refs, prefix_refs = refs[known + PLANE : -PLANE], refs[-PLANE:]
    earlier = sum_of_earlier(unit, got_refs)
    for known_ref in known_refs:
        earlier = earlier + known_ref[...]
    shares = [share_ref[...].astype(F32) for share_ref in share_refs]
    for piece, prefix_ref in enumerate(prefix_refs):
        prefix = earlier
        for other in range(PLANE):
            if other != piece:
                ahead = (chip ^ other) < (chip ^ piece)
                prefix = prefix + jnp.where(ahead, shares[other], 0.0)
        prefix_ref[...] = prefix.astype(BF16)


def stack_kernel(*refs):
    piece_refs, all_ref = refs[:-1], refs[-1]
    for piece, piece_ref in enumerate(piece_refs):
        all_ref[piece] = piece_ref[...]


def earlier_chips(keep, send):
    devices = lax.axis_size("seq")
    dims = keep.shape[1:]
    wide, narrow = pltpu.VMEM(dims, F32), pltpu.VMEM(dims, BF16)
    own, *sent = kernel_call(
        chip_sum_kernel, (wide,) + (narrow,) * (PLANE - 1), keep, swap(send, 1)
    )
    shares = [own] + [swap(block, CORES * m) for m, block in enumerate(sent, 1)]
    unit, known = CORES * PLANE, ()
    radix = min(RADIX, devices // unit)
    shapes = (narrow,) if unit * radix >= devices else (narrow, wide)
    block, *total = kernel_call(plane_sum_kernel, shapes, *shares)
    while True:
        got = [swap(block, unit * m) for m in range(1, radix)]
        if unit * radix >= devices:
            break
        next_radix = min(RADIX, devices // (unit * radix))
        shapes = (narrow,) if unit * radix * next_radix >= devices else (narrow, wide)
        earlier, block, *total = kernel_call(
            functools.partial(across_kernel, unit, len(known), radix),
            (wide,) + shapes,
            *total,
            *known,
            *got,
        )
        unit, known, radix = unit * radix, (earlier,), next_radix
    prefixes = kernel_call(
        functools.partial(prefix_kernel, unit, len(known)), (narrow,) * PLANE, *known, *shares, *got
    )
    mine = kernel_call(
        stack_kernel,
        pltpu.VMEM((PLANE,) + dims, BF16),
        prefixes[0],
        *[swap(prefixes[m], CORES * m) for m in range(1, PLANE)],
    )
    return mine, swap(mine, 1)


def block_program(queries, keys, values, out_gain, hash_ids, sign_ids):
    rows, width = queries.shape
    heads = width // HD
    half_heads = heads // 2
    half_state = pltpu.VMEM((PLANE, heads // (CORES * PLANE), FEATURES, HD), F32)
    half_rows = pltpu.VMEM((rows, width // 2), BF16)
    half_near = pltpu.VMEM((rows, width // 2), F32)
    id_shape = pltpu.VMEM(hash_ids.shape, hash_ids.dtype)

    send, keep, hash_near, sign_near, query_0, query_1, key_0, key_1, value_0, value_1 = kernel_call(
        state_kernel,
        (half_state, half_state, id_shape, id_shape) + (half_rows,) * 6,
        hash_ids,
        sign_ids,
        queries,
        keys,
        values,
        space=pltpu.HBM,
        in_specs=[IN_HBM] * 5,
        scratch_shapes=[pltpu.SemaphoreType.DMA((10,))],
    )
    key_prev = from_behind(keys, closed=True)
    value_prev_1 = from_behind(value_0, closed=True)
    value_prev_0 = from_behind(value_1)
    mine, theirs = earlier_chips(keep, send)
    phi = kernel_call(
        query_kernel,
        pltpu.VMEM((heads, rows, FEATURES), BF16),
        hash_near,
        sign_near,
        query_0,
        query_1,
    )
    near = []
    for half, query, key, value, value_prev in (
        (0, query_0, key_0, value_0, value_prev_0),
        (1, query_1, key_1, value_1, value_prev_1),
    ):
        own = kernel_call(own_kernel, half_near, query, key, value)
        weights = kernel_call(
            functools.partial(weights_kernel, half),
            pltpu.VMEM((half_heads, rows, rows), BF16),
            hash_near,
            sign_near,
            query,
            key_prev,
        )
        near.append(kernel_call(values_kernel, half_near, weights, value_prev, own))
    return kernel_call(
        far_kernel,
        pltpu.HBM((rows, width), BF16),
        phi,
        theirs,
        mine,
        *near,
        out_gain.reshape(1, width),
        out_specs=IN_HBM,
        scratch_shapes=[
            pltpu.VMEM((CORES * PLANE, rows, width // (CORES * PLANE)), BF16),
            pltpu.SemaphoreType.DMA((CORES * PLANE,)),
        ],
    )


def solution(mesh):
    in_specs = (
        P(("grp", "seq"), "head"),
        P(("grp", "seq"), "head"),
        P(("grp", "seq"), "head"),
        P("head"),
        P(),
        P(),
    )
    out_specs = P(("grp", "seq"), "head")
    return jax.shard_map(
        block_program, mesh=mesh, in_specs=in_specs, out_specs=out_specs, check_vma=False
    )
```
